1024 devices in a mesh: section: 8 (over y_lo, x), half: 2 (over y_hi), dp: 64 (over z, core).
Axes of the slice: x: 4, y: 4 (y_hi: 2, y_lo: 2; y = y_hi * 2 + y_lo), z: 32, core: 2. Of those that a mesh axis runs over, the one named last changes fastest.
Arguments:
- query: bfloat16 [1024, 24576], P('dp', ('section', 'half')), may hold values from -6 to 6
- train: bfloat16 [65536, 24576], P('dp', ('section', 'half')), may hold values from -0.0390625 to 0.0390625
- precond: bfloat16 [96, 256, 256], P(('section', 'half')), may hold values from -0.375 to 0.375
- module_kind: int32 [96], P(('section', 'half')), may hold values from 0 to 6
- kind_scale: float32 [7], replicated, may hold values from 0.25 to 4
Outputs:
- scores: float32 [1024, 65536], P(('section', 'half'), 'dp')
The draws below stay inside these ranges and needn't reach their ends.
All inputs are finite; a program needn't handle non-finite values.
Results may differ from the reference program's by a relative error of at most 0.0029.
Values may be sent and summed in bfloat16 or wider, within the bound.
A program may use at most 32 MiB of HBM per device.

```python
import math
import jax
import jax.numpy as jnp
from jax import lax

FEAT = 256
KINDS = 7
MODULES = 96
FEATURES = 24576
TRAIN = 65536
Q = 1024


def with_ends(values, key, low, largest):
    extent = values.shape
    index_at = [jax.random.randint(jax.random.fold_in(key, axis), (), 0, extent[axis]) for axis in range(len(extent))]
    values = values.at[tuple(index_at)].set(low)
    longest = extent.index(max(extent))
    index_at[longest] = (index_at[longest] + 1) % extent[longest]
    return values.at[tuple(index_at)].set(largest)


def shard_levels(rng, shape, cuts, least, high):
    def one(dim, blocks):
        steps = jax.random.uniform(jax.random.fold_in(jax.random.fold_in(rng, 6), dim), (blocks,), jnp.float32, least / len(cuts), high / len(cuts))
        return jnp.repeat(jnp.exp(steps), shape[dim] // blocks).reshape((-1,) + (1,) * (len(shape) - dim - 1))

    gain = one(*cuts[0])
    for cut in cuts[1:]:
        gain = gain * one(*cut)
    return gain


def centred(own_key, dims, scale, most, shards=(), kind=jnp.bfloat16):
    result = jax.random.normal(own_key, dims, jnp.float32) * scale
    if len(shards) > 0:
        result = shard_levels(own_key, dims, shards, -0.22, 0.18) * result
    return jnp.clip(result, min=-most, max=most).astype(kind)


def setup_inputs(seed: int = 0) -> dict:
    key_list = jax.random.split(jax.random.key(seed), 6)
    query = centred(key_list[0], (Q, FEATURES), 1.0, 6.0, ((0, 64), (1, 16)))
    train = centred(key_list[1], (TRAIN, FEATURES), FEATURES ** -0.5, 0.0390625, ((0, 64), (1, 16)))
    precond = centred(key_list[2], (MODULES, FEAT, FEAT), FEAT ** -0.5, 0.375, ((0, 16),))
    module_kind = with_ends(jax.random.randint(key_list[3], (MODULES,), 0, KINDS), jax.random.fold_in(key_list[3], 1), 0, KINDS - 1).astype(jnp.int32)
    kind_scale = jnp.clip(jnp.exp(jax.random.uniform(key_list[4], (KINDS,), jnp.float32, math.log(0.25), math.log(4.0))), 0.25, 4.0)
    return {"query": query, "train": train, "precond": precond, "module_kind": module_kind, "kind_scale": kind_scale}


def reference(query, train, precond, module_kind, kind_scale):
    blocks = query.astype(jnp.float32).reshape(Q, MODULES, FEAT)
    pre = jnp.einsum("qmf,mfg->qmg", blocks, precond.astype(jnp.float32), precision=lax.Precision.HIGHEST)
    kinds = jnp.arange(KINDS, dtype=jnp.int32)
    onehot = (module_kind[:, None] == kinds[None, :]).astype(jnp.float32)
    factor = jnp.sum(onehot * kind_scale[None, :], axis=1)
    weighted = (pre * factor[None, :, None]).astype(jnp.bfloat16).reshape(Q, FEATURES)
    return lax.dot_general(weighted, train, (((1,), (1,)), ((), ())), preferred_element_type=jnp.float32)
```

```python
import jax
import jax.numpy as jnp
from jax import lax
from jax.experimental import pallas as pl
from jax.experimental.pallas import tpu as pltpu
from jax.sharding import PartitionSpec as P

MESH = pl.DeviceIdType.MESH
PIECES = 3
STRIDE = 3
SIDE = 4


def kernel(
    kind_ref, scale_ref, query_hbm, pre_hbm, train_hbm, out_ref,
    q_v, pre_v, t_v, w_v, s_v, a_v, own_v, g_v, r_v,
    in_sem, ring_send, chain_recv, fill_recv, sib_send, sib_recv, first_send, first_recv, second_send, second_recv,
):
    dp = lax.axis_index("dp")
    sec = lax.axis_index("section")
    half = lax.axis_index("half")
    chips = lax.axis_size("dp") // 2
    halves = lax.axis_size("half")
    owners = lax.axis_size("section") * halves
    share = chips // owners
    me = sec * halves + half
    z = dp // 2
    core = dp % 2
    sign = 1 - 2 * core
    x = sec % SIDE
    y = half * (SIDE // halves) + sec // SIDE
    rows = q_v.shape[0]
    mods, feat, _ = pre_v.shape
    width = w_v.shape[2]
    cols = t_v.shape[0] // SIDE
    both = 2 * rows
    last = chips // 2
    turns = 5 if STRIDE == 3 else 7

    def chip(step):
        return (z + step + 2 * chips) % chips

    def at_xy(px, py):
        low = SIDE // halves
        return {"section": (py % low) * SIDE + px, "half": py // low}

    def along(way, delta):
        return {"dp": chip(sign * delta if way == 0 else -sign * delta) * 2 + core}

    def origin(way, r):
        return chip(-sign * r if way == 0 else sign * r)

    sibling = {"dp": z * 2 + 1 - core}

    load_q = pltpu.make_async_copy(query_hbm, q_v, in_sem.at[0])
    load_pre = pltpu.make_async_copy(pre_hbm, pre_v, in_sem.at[1])
    load_t = pltpu.make_async_copy(train_hbm, t_v, in_sem.at[2])
    load_q.start()
    load_pre.start()
    load_t.start()

    barrier = pltpu.get_barrier_semaphore()
    near = [along(0, 1), along(1, 1), along(0, STRIDE), along(1, STRIDE), sibling]
    for target in near:
        pl.semaphore_signal(barrier, inc=1, device_id=target, device_id_type=MESH)

    def greet(step, carry):
        other = (me + step) % owners
        pl.semaphore_signal(
            barrier, inc=1, device_id={"section": other // halves, "half": other % halves}, device_id_type=MESH)
        return carry

    lax.fori_loop(1, owners, greet, 0)

    load_q.wait()
    load_pre.wait()
    mine = pl.ds(pl.multiple_of(dp * rows, rows), rows)
    for m in range(mods):
        factor = scale_ref[kind_ref[m]]
        pre = jnp.dot(q_v[:, m * feat:(m + 1) * feat], pre_v[m], preferred_element_type=jnp.float32)
        first = m * feat
        w_v[first // width, mine, first % width:first % width + feat] = (pre * factor).astype(jnp.bfloat16)
    pl.semaphore_wait(barrier, owners - 1 + len(near))

    def block(c, lane):
        return pl.ds(pl.multiple_of((c * 2 + lane) * rows, rows), rows)

    def chain(way, r, piece):
        at = w_v.at[piece, block(origin(way, r - STRIDE), core)]
        return pltpu.make_async_remote_copy(
            src_ref=at, dst_ref=at, send_sem=ring_send.at[way], recv_sem=chain_recv.at[way, r, piece],
            device_id=along(way, STRIDE), device_id_type=MESH)

    def chain_wait(way, r, piece):
        at = w_v.at[piece, block(origin(way, r), core)]
        pltpu.make_async_remote_copy(
            src_ref=at, dst_ref=at, send_sem=ring_send.at[way], recv_sem=chain_recv.at[way, r, piece],
            device_id=along(way, STRIDE), device_id_type=MESH).wait_recv()

    def fill(way, r, delta):
        at = w_v.at[:, block(origin(way, r - delta), core)]
        return pltpu.make_async_remote_copy(
            src_ref=at, dst_ref=at, send_sem=ring_send.at[way], recv_sem=fill_recv.at[way, r],
            device_id=along(way, delta), device_id_type=MESH)

    def fill_wait(way, r):
        at = w_v.at[:, block(origin(way, r), core)]
        pltpu.make_async_remote_copy(
            src_ref=at, dst_ref=at, send_sem=ring_send.at[way], recv_sem=fill_recv.at[way, r],
            device_id=along(way, 1), device_id_type=MESH).wait_recv()

    def across(way, r):
        at = w_v.at[:, block(origin(way, r), core)]
        pltpu.make_async_remote_copy(
            src_ref=at, dst_ref=at, send_sem=sib_send, recv_sem=sib_recv.at[way, r],
            device_id=sibling, device_id_type=MESH).start()

    def across_wait(way, r):
        at = w_v.at[:, block(origin(1 - way, r), 1 - core)]
        pltpu.make_async_remote_copy(
            src_ref=at, dst_ref=at, send_sem=sib_send, recv_sem=sib_recv.at[way, r],
            device_id=sibling, device_id_type=MESH).wait_recv()

    def relay(r, ways, on, up, down):
        for piece in range(PIECES):
            for way in ways:
                chain_wait(way, r, piece)
                if way in on:
                    chain(way, r + STRIDE, piece).start()
        for way in ways:
            if way in up:
                fill(way, r + 1, 1).start()
            if way in down:
                fill(way, r - 1, -1).start()
            across(way, r)

    def filled(ways, r):
        for way in ways:
            fill_wait(way, r)
            across(way, r)

    def peer(way, d):
        return at_xy((x + d) % SIDE, y) if way == 0 else at_xy(x, (y + d) % SIDE)

    def first(batch, way, d, n):
        return pltpu.make_async_remote_copy(
            src_ref=s_v.at[batch, way, d - 1, pl.ds(0, n * both)],
            dst_ref=a_v.at[batch, way, d - 1, pl.ds(0, n * both)],
            send_sem=first_send, recv_sem=first_recv.at[batch, way, d - 1],
            device_id=peer(way, d), device_id_type=MESH)

    def multiply(batch, lists):
        for way in range(2):
            for r in lists[way]:
                shared = isinstance(r, int) and r in (0, last)
                across_wait(0 if shared else 1 - way, r)
        for way in range(2):
            chunks = [origin(way, r) for r in lists[way]]
            n = len(chunks)
            lhs = []
            for piece in range(PIECES):
                parts = [w_v[piece, pl.ds(pl.multiple_of(c * both, both), both), :] for c in chunks]
                lhs.append(jnp.concatenate(parts, axis=0) if n > 1 else parts[0])
            for d in (2, 1, 3, 0):
                quarter = ((x if way == 0 else y) + d) % SIDE
                total = None
                for piece in range(PIECES):
                    part = lax.dot_general(
                        lhs[piece],
                        t_v[pl.ds(pl.multiple_of(quarter * cols, cols), cols), piece * width:(piece + 1) * width],
                        (((1,), (1,)), ((), ())), preferred_element_type=jnp.float32)
                    total = part if total is None else total + part
                if d:
                    s_v[batch, way, d - 1, 0:n * both, :] = total.astype(jnp.bfloat16)
                    first(batch, way, d, n).start()
                else:
                    own_v[batch, way, 0:n * both, :] = total

    def reduce(batch, lists):
        for way in range(2):
            n = len(lists[way])
            total = own_v[batch, way, 0:n * both, :]
            for d in (1, 3, 2):
                first(batch, way, d, n).wait_recv()
                total += a_v[batch, way, d - 1, 0:n * both, :].astype(jnp.float32)
            g_v[batch, way, 0:n * both, :] = total.astype(jnp.bfloat16)
            for k, r in enumerate(lists[way]):
                c = origin(way, r)
                owner = c // share
                e = c % share
                quarter, other = (x, y) if way == 0 else (y, x)
                here = pl.ds(k * both, both)

                @pl.when(owner == me)
                def _():
                    r_v[e, quarter, other] = g_v[batch, way, here, :]

                @pl.when(owner != me)
                def _():
                    pltpu.make_async_remote_copy(
                        src_ref=g_v.at[batch, way, here], dst_ref=r_v.at[e, quarter, other],
                        send_sem=second_send, recv_sem=second_recv.at[e, quarter, other],
                        device_id={"section": owner // halves, "half": owner % halves},
                        device_id_type=MESH).start()

    for piece in range(PIECES):
        for way in range(2):
            chain(way, STRIDE, piece).start()
    for way in range(2):
        fill(way, 1, 1).start()
    across(0, 0)

    w01 = (0, 1)
    three = STRIDE == 3

    def batch_of(m):
        rs = [STRIDE * m - 1, STRIDE * m, STRIDE * m + 1] if three else [STRIDE * m, STRIDE * m + 1]
        return [rs, rs]

    head = [[0, 1], [1]]
    tail = [[last - 2, last - 1, last], [last - 2, last - 1]]
    down = w01 if three else ()

    filled(w01, 1)
    relay(STRIDE, w01, w01, w01, down)
    load_t.wait()
    multiply(0, head)

    def turn(j, carry):
        if three:
            filled(w01, STRIDE * (j - 1) - 1)
        filled(w01, STRIDE * (j - 1) + 1)
        relay(STRIDE * j, w01, w01, w01, down)
        multiply(j - 1, batch_of(j - 1))

        @pl.when(j == 2)
        def _():
            reduce(0, head)

        @pl.when(j > 2)
        def _():
            reduce(j - 2, batch_of(j - 2))
        return carry

    lax.fori_loop(2, turns, turn, 0)
    j = turns
    if three:
        filled(w01, STRIDE * (j - 1) - 1)
    filled(w01, STRIDE * (j - 1) + 1)
    if three:
        relay(STRIDE * j, w01, (), (0,), w01)
    else:
        relay(STRIDE * j, w01, (0,), w01, ())
    multiply(j - 1, batch_of(j - 1))
    reduce(j - 2, batch_of(j - 2))
    if three:
        filled(w01, last - 2)
        filled((0,), last)
    else:
        filled(w01, last - 1)
        relay(last, (0,), (), (), ())
    multiply(j, tail)
    reduce(j - 1, batch_of(j - 1))
    reduce(j, tail)

    def collect(i, carry):
        e, quarter, other = i // owners, (i // SIDE) % SIDE, i % SIDE
        c = me * share + e
        step = (c - z + chips) % chips
        ahead = (step * sign + 2 * chips) % chips
        to_x = jnp.where((ahead == 0) | (ahead >= last), 1, 0)
        source_x = to_x * quarter + (1 - to_x) * other
        source_y = to_x * other + (1 - to_x) * quarter

        @pl.when((source_x != x) | (source_y != y))
        def _():
            pltpu.make_async_remote_copy(
                src_ref=r_v.at[e, quarter, other], dst_ref=r_v.at[e, quarter, other],
                send_sem=second_send, recv_sem=second_recv.at[e, quarter, other],
                device_id=sibling, device_id_type=MESH).wait_recv()
        return carry

    lax.fori_loop(0, share * owners, collect, 0)
    for e in range(share):
        for quarter in range(SIDE):
            total = r_v[e, quarter, 0].astype(jnp.float32)
            for other in range(1, SIDE):
                total += r_v[e, quarter, other].astype(jnp.float32)
            out_ref[e * both:(e + 1) * both, quarter * cols:(quarter + 1) * cols] = total

    def sent(ref, sem):
        pltpu.make_async_copy(ref, ref, sem).wait()

    total_rows = chips * both
    sent(w_v.at[:, pl.ds(0, last * rows)], ring_send.at[0])
    sent(w_v.at[:, pl.ds(0, (last - 1) * rows)], ring_send.at[1])
    sent(w_v.at[:, pl.ds(0, chips * rows)], sib_send)
    sent(w_v.at[:, pl.ds(0, total_rows // 2)], first_send)
    sent(w_v.at[0, pl.ds(0, (chips - share) * both // 2)], second_send)


def per_device(query, train, precond, module_kind, kind_scale):
    rows, features = query.shape
    cols = train.shape[0] // SIDE
    devices = lax.axis_size("dp")
    owners = lax.axis_size("section") * lax.axis_size("half")
    total = devices * rows
    share = devices // 2 // owners
    batches = 6 if STRIDE == 3 else 8
    half = devices // 4 + 1
    group = 3 * 2 * rows
    return pl.pallas_call(
        kernel,
        out_shape=jax.ShapeDtypeStruct((total // owners, train.shape[0]), jnp.float32),
        in_specs=[
            pl.BlockSpec(memory_space=pltpu.SMEM),
            pl.BlockSpec(memory_space=pltpu.SMEM),
            pl.BlockSpec(memory_space=pl.ANY),
            pl.BlockSpec(memory_space=pl.ANY),
            pl.BlockSpec(memory_space=pl.ANY),
        ],
        out_specs=pl.BlockSpec(memory_space=pltpu.VMEM),
        scratch_shapes=[
            pltpu.VMEM(query.shape, jnp.bfloat16),
            pltpu.VMEM(precond.shape, jnp.bfloat16),
            pltpu.VMEM(train.shape, jnp.bfloat16),
            pltpu.VMEM((PIECES, total, features // PIECES), jnp.bfloat16),
            pltpu.VMEM((batches, 2, SIDE - 1, group, cols), jnp.bfloat16),
            pltpu.VMEM((batches, 2, SIDE - 1, group, cols), jnp.bfloat16),
            pltpu.VMEM((batches, 2, group, cols), jnp.float32),
            pltpu.VMEM((batches, 2, group, cols), jnp.bfloat16),
            pltpu.VMEM((share, SIDE, SIDE, 2 * rows, cols), jnp.bfloat16),
            pltpu.SemaphoreType.DMA((3,)),
            pltpu.SemaphoreType.DMA((2,)),
            pltpu.SemaphoreType.DMA((2, half, PIECES)),
            pltpu.SemaphoreType.DMA((2, half)),
            pltpu.SemaphoreType.DMA,
            pltpu.SemaphoreType.DMA((2, half)),
            pltpu.SemaphoreType.DMA,
            pltpu.SemaphoreType.DMA((batches, 2, SIDE - 1)),
            pltpu.SemaphoreType.DMA,
            pltpu.SemaphoreType.DMA((share, SIDE, SIDE)),
        ],
        compiler_params=pltpu.CompilerParams(
            collective_id=0, has_side_effects=True, vmem_limit_bytes=48 * 1024 * 1024),
    )(module_kind, kind_scale, query, precond, train)


def solution(mesh):
    in_specs = (
        P("dp", ("section", "half")),
        P("dp", ("section", "half")),
        P(("section", "half"), None, None),
        P(("section", "half")),
        P(),
    )
    out_specs = P(("section", "half"), "dp")
    return jax.shard_map(
        per_device, mesh=mesh, in_specs=in_specs, out_specs=out_specs, check_vma=False
    )
```

```python
import jax
import jax.numpy as jnp
from jax import lax
from jax.experimental import pallas as pl
from jax.experimental.pallas import tpu as pltpu
from jax.sharding import PartitionSpec as P

MESH = pl.DeviceIdType.MESH
PIECES = 3
STRIDE = 3
TURNS = 5
SIDE = 4


def kernel(
    kind_hbm, scale_hbm, query_hbm, pre_hbm, train_hbm, r_hbm,
    kind_ref, scale_ref, q_v, pre_v, t_v, w_v, s_v, a_v, own_v, g_v,
    in_sem, ring_send, chain_recv, fill_recv, sib_send, sib_recv, first_send, first_recv, second_send, second_recv,
):
    dp = lax.axis_index("dp")
    sec = lax.axis_index("section")
    half = lax.axis_index("half")
    chips = lax.axis_size("dp") // 2
    halves = lax.axis_size("half")
    owners = lax.axis_size("section") * halves
    share = chips // owners
    me = sec * halves + half
    z = dp // 2
    core = dp % 2
    sign = 1 - 2 * core
    x = sec % SIDE
    y = half * (SIDE // halves) + sec // SIDE
    rows = q_v.shape[0]
    mods, feat, _ = pre_v.shape
    width = w_v.shape[2]
    cols = t_v.shape[0] // SIDE
    both = 2 * rows
    last = chips // 2

    def chip(step):
        return (z + step + 2 * chips) % chips

    def at_xy(px, py):
        low = SIDE // halves
        return {"section": (py % low) * SIDE + px, "half": py // low}

    def along(way, delta):
        return {"dp": chip(sign * delta if way == 0 else -sign * delta) * 2 + core}

    def beyond(way, delta):
        return {"dp": chip(sign * delta if way == 0 else -sign * delta) * 2 + 1 - core}

    def origin(way, r):
        return chip(-sign * r if way == 0 else sign * r)

    sibling = {"dp": z * 2 + 1 - core}

    load_q = pltpu.make_async_copy(query_hbm, q_v, in_sem.at[0])
    load_pre = pltpu.make_async_copy(pre_hbm, pre_v, in_sem.at[1])
    load_t = pltpu.make_async_copy(train_hbm, t_v, in_sem.at[2])
    load_kind = pltpu.make_async_copy(kind_hbm, kind_ref, in_sem.at[3])
    load_scale = pltpu.make_async_copy(scale_hbm, scale_ref, in_sem.at[4])
    load_q.start()
    load_kind.start()
    load_scale.start()
    load_pre.start()
    load_t.start()

    barrier = pltpu.get_barrier_semaphore()
    near = [along(0, 1), along(1, 1), along(0, STRIDE), along(1, STRIDE), sibling, beyond(0, 1), beyond(1, 1)]
    for target in near:
        pl.semaphore_signal(barrier, inc=1, device_id=target, device_id_type=MESH)

    def greet(step, carry):
        other = (me + step) % owners
        pl.semaphore_signal(
            barrier, inc=1, device_id={"section": other // halves, "half": other % halves}, device_id_type=MESH)
        return carry

    lax.fori_loop(1, owners, greet, 0)

    load_q.wait()
    load_kind.wait()
    load_scale.wait()
    load_pre.wait()
    mine = pl.ds(pl.multiple_of(dp * rows, rows), rows)
    for m in range(mods):
        factor = scale_ref[kind_ref[m]]
        pre = jnp.dot(q_v[:, m * feat:(m + 1) * feat], pre_v[m], preferred_element_type=jnp.float32)
        first = m * feat
        w_v[first // width, mine, first % width:first % width + feat] = (pre * factor).astype(jnp.bfloat16)
    pl.semaphore_wait(barrier, owners - 1 + len(near))

    def block(c, lane):
        return pl.ds(pl.multiple_of((c * 2 + lane) * rows, rows), rows)

    def chain(way, r, piece):
        at = w_v.at[piece, block(origin(way, r - STRIDE), core)]
        return pltpu.make_async_remote_copy(
            src_ref=at, dst_ref=at, send_sem=ring_send.at[way], recv_sem=chain_recv.at[way, r, piece],
            device_id=along(way, STRIDE), device_id_type=MESH)

    def chain_wait(way, r, piece):
        at = w_v.at[piece, block(origin(way, r), core)]
        pltpu.make_async_remote_copy(
            src_ref=at, dst_ref=at, send_sem=ring_send.at[way], recv_sem=chain_recv.at[way, r, piece],
            device_id=along(way, STRIDE), device_id_type=MESH).wait_recv()

    def fill(way, r, delta):
        at = w_v.at[:, block(origin(way, r - delta), core)]
        return pltpu.make_async_remote_copy(
            src_ref=at, dst_ref=at, send_sem=ring_send.at[way], recv_sem=fill_recv.at[way, r],
            device_id=along(way, delta), device_id_type=MESH)

    def fill_wait(way, r):
        at = w_v.at[:, block(origin(way, r), core)]
        pltpu.make_async_remote_copy(
            src_ref=at, dst_ref=at, send_sem=ring_send.at[way], recv_sem=fill_recv.at[way, r],
            device_id=along(way, 1), device_id_type=MESH).wait_recv()

    def across(way, r):
        at = w_v.at[:, block(origin(way, r), core)]
        pltpu.make_async_remote_copy(
            src_ref=at, dst_ref=at, send_sem=sib_send, recv_sem=sib_recv.at[way, r],
            device_id=sibling, device_id_type=MESH).start()

    def cross(way, r, delta):
        at = w_v.at[:, block(origin(way, r - delta), core)]
        pltpu.make_async_remote_copy(
            src_ref=at, dst_ref=at, send_sem=sib_send, recv_sem=sib_recv.at[way, r],
            device_id=beyond(way, delta), device_id_type=MESH).start()

    def across_wait(way, r):
        at = w_v.at[:, block(origin(1 - way, r), 1 - core)]
        pltpu.make_async_remote_copy(
            src_ref=at, dst_ref=at, send_sem=sib_send, recv_sem=sib_recv.at[way, r],
            device_id=sibling, device_id_type=MESH).wait_recv()

    def relay(r, ways, on, up, down):
        for piece in range(PIECES):
            for way in ways:
                chain_wait(way, r, piece)
                if way in on:
                    chain(way, r + STRIDE, piece).start()
        for way in ways:
            if way in up:
                fill(way, r + 1, 1).start()
            if way in down:
                fill(way, r - 1, -1).start()
            across(way, r)

    def filled(ways, r):
        for way in ways:
            fill_wait(way, r)
            across(way, r)

    def peer(way, d):
        return at_xy((x + d) % SIDE, y) if way == 0 else at_xy(x, (y + d) % SIDE)

    def first(batch, way, d, n):
        return pltpu.make_async_remote_copy(
            src_ref=s_v.at[batch, way, d - 1, pl.ds(0, n * both)],
            dst_ref=a_v.at[batch, way, d - 1, pl.ds(0, n * both)],
            send_sem=first_send, recv_sem=first_recv.at[batch, way, d - 1],
            device_id=peer(way, d), device_id_type=MESH)

    def multiply(batch, lists):
        for way in range(2):
            for r in lists[way]:
                shared = isinstance(r, int) and r in (0, last)
                across_wait(0 if shared else 1 - way, r)
        for way in range(2):
            chunks = [origin(way, r) for r in lists[way]]
            n = len(chunks)
            lhs = []
            for piece in range(PIECES):
                parts = [w_v[piece, pl.ds(pl.multiple_of(c * both, both), both), :] for c in chunks]
                lhs.append(jnp.concatenate(parts, axis=0) if n > 1 else parts[0])
            for d in (2, 1, 3, 0):
                quarter = ((x if way == 0 else y) + d) % SIDE
                total = None
                for piece in range(PIECES):
                    part = lax.dot_general(
                        lhs[piece],
                        t_v[pl.ds(pl.multiple_of(quarter * cols, cols), cols), piece * width:(piece + 1) * width],
                        (((1,), (1,)), ((), ())), preferred_element_type=jnp.float32)
                    total = part if total is None else total + part
                if d:
                    s_v[batch, way, d - 1, 0:n * both, :] = total.astype(jnp.bfloat16)
                    first(batch, way, d, n).start()
                else:
                    own_v[batch, way, 0:n * both, :] = total

    def reduce(batch, lists):
        for way in range(2):
            n = len(lists[way])
            total = own_v[batch, way, 0:n * both, :]
            for d in (1, 3, 2):
                first(batch, way, d, n).wait_recv()
                total += a_v[batch, way, d - 1, 0:n * both, :].astype(jnp.float32)
            g_v[batch, way, 0:n * both, :] = total.astype(jnp.bfloat16)
            for k, r in enumerate(lists[way]):
                c = origin(way, r)
                owner = c // share
                e = c % share
                quarter, other = (x, y) if way == 0 else (y, x)
                here = pl.ds(k * both, both)

                slot = r_hbm.at[
                    other, pl.ds(pl.multiple_of(e * both, both), both),
                    pl.ds(pl.multiple_of(quarter * cols, cols), cols)]

                @pl.when(owner == me)
                def _():
                    pltpu.make_async_copy(g_v.at[batch, way, here], slot, in_sem.at[5]).start()

                @pl.when(owner != me)
                def _():
                    pltpu.make_async_remote_copy(
                        src_ref=g_v.at[batch, way, here], dst_ref=slot,
                        send_sem=second_send, recv_sem=second_recv.at[e, quarter, other],
                        device_id={"section": owner // halves, "half": owner % halves},
                        device_id_type=MESH).start()

    for piece in range(PIECES):
        for way in range(2):
            chain(way, STRIDE, piece).start()
    for way in range(2):
        fill(way, 1, 1).start()
    across(0, 0)

    w01 = (0, 1)

    def batch_of(j):
        rs = [STRIDE * j - 4, STRIDE * j - 2, STRIDE * j]
        return [rs, rs]

    head = [[0, 1, STRIDE], [1, STRIDE]]
    tail = [[last - 2, last], [last - 2]]

    relay(STRIDE, w01, w01, w01, w01)
    filled(w01, 1)
    relay(STRIDE * 2, w01, w01, w01, w01)
    load_t.wait()
    multiply(0, head)
    filled(w01, STRIDE * 2 - 4)
    filled(w01, STRIDE * 2 - 2)

    def turn(j, carry):
        relay(STRIDE * j, w01, w01, w01, w01)
        multiply(j - 2, batch_of(j - 1))

        @pl.when(j == 3)
        def _():
            reduce(0, head)

        @pl.when(j > 3)
        def _():
            reduce(j - 3, batch_of(j - 2))
        filled(w01, STRIDE * j - 4)
        filled(w01, STRIDE * j - 2)
        return carry

    lax.fori_loop(3, TURNS, turn, 0)
    j = TURNS
    relay(STRIDE * j, w01, (), (0,), w01)
    cross(0, last, 1)
    cross(0, last - 2, -1)
    cross(1, last - 2, -1)
    filled(w01, STRIDE * j - 4)
    filled(w01, STRIDE * j - 2)
    multiply(j - 2, batch_of(j - 1))
    reduce(j - 3, batch_of(j - 2))
    multiply(j - 1, batch_of(j))
    reduce(j - 2, batch_of(j - 1))
    for way, r in ((0, last), (0, last - 2), (1, last - 2)):
        fill_wait(way, r)
    multiply(j, tail)
    reduce(j - 1, batch_of(j))
    reduce(j, tail)

    def collect(i, carry):
        e, quarter, other = i // owners, (i // SIDE) % SIDE, i % SIDE
        c = me * share + e
        step = (c - z + chips) % chips
        ahead = (step * sign + 2 * chips) % chips
        to_x = jnp.where((ahead == 0) | (ahead >= last), 1, 0)
        source_x = to_x * quarter + (1 - to_x) * other
        source_y = to_x * other + (1 - to_x) * quarter

        @pl.when((source_x != x) | (source_y != y))
        def _():
            slot = r_hbm.at[
                other, pl.ds(pl.multiple_of(e * both, both), both),
                pl.ds(pl.multiple_of(quarter * cols, cols), cols)]
            pltpu.make_async_remote_copy(
                src_ref=slot, dst_ref=slot,
                send_sem=second_send, recv_sem=second_recv.at[e, quarter, other],
                device_id=sibling, device_id_type=MESH).wait_recv()
        return carry

    lax.fori_loop(0, share * owners, collect, 0)
    def sent(ref, sem):
        pltpu.make_async_copy(ref, ref, sem).wait()

    total_rows = chips * both
    sent(g_v.at[0, 0, pl.ds(0, share * both)], in_sem.at[5])
    sent(w_v.at[:, pl.ds(0, last * rows)], ring_send.at[0])
    sent(w_v.at[:, pl.ds(0, (last - 1) * rows)], ring_send.at[1])
    sent(w_v.at[:, pl.ds(0, chips * rows)], sib_send)
    sent(w_v.at[:, pl.ds(0, total_rows // 2)], first_send)
    sent(w_v.at[0, pl.ds(0, (chips - share) * both * cols // width)], second_send)


def per_device(query, train, precond, module_kind, kind_scale):
    rows, features = query.shape
    cols = train.shape[0] // SIDE
    devices = lax.axis_size("dp")
    owners = lax.axis_size("section") * lax.axis_size("half")
    total = devices * rows
    share = devices // 2 // owners
    batches = TURNS + 1
    half = devices // 4 + 1
    group = 3 * 2 * rows
    parts = pl.pallas_call(
        kernel,
        out_shape=jax.ShapeDtypeStruct((SIDE, total // owners, train.shape[0]), jnp.bfloat16),
        in_specs=[
            pl.BlockSpec(memory_space=pltpu.HBM),
            pl.BlockSpec(memory_space=pltpu.HBM),
            pl.BlockSpec(memory_space=pltpu.HBM),
            pl.BlockSpec(memory_space=pltpu.HBM),
            pl.BlockSpec(memory_space=pltpu.HBM),
        ],
        out_specs=pl.BlockSpec(memory_space=pltpu.HBM),
        scratch_shapes=[
            pltpu.SMEM(module_kind.shape, jnp.int32),
            pltpu.SMEM(kind_scale.shape, jnp.float32),
            pltpu.VMEM(query.shape, jnp.bfloat16),
            pltpu.VMEM(precond.shape, jnp.bfloat16),
            pltpu.VMEM(train.shape, jnp.bfloat16),
            pltpu.VMEM((PIECES, total, features // PIECES), jnp.bfloat16),
            pltpu.VMEM((batches, 2, SIDE - 1, group, cols), jnp.bfloat16),
            pltpu.VMEM((batches, 2, SIDE - 1, group, cols), jnp.bfloat16),
            pltpu.VMEM((batches, 2, group, cols), jnp.float32),
            pltpu.VMEM((batches, 2, group, cols), jnp.bfloat16),
            pltpu.SemaphoreType.DMA((6,)),
            pltpu.SemaphoreType.DMA((2,)),
            pltpu.SemaphoreType.DMA((2, half, PIECES)),
            pltpu.SemaphoreType.DMA((2, half)),
            pltpu.SemaphoreType.DMA,
            pltpu.SemaphoreType.DMA((2, half)),
            pltpu.SemaphoreType.DMA,
            pltpu.SemaphoreType.DMA((batches, 2, SIDE - 1)),
            pltpu.SemaphoreType.DMA,
            pltpu.SemaphoreType.DMA((share, SIDE, SIDE)),
        ],
        compiler_params=pltpu.CompilerParams(
            collective_id=0, has_side_effects=True, vmem_limit_bytes=67043328),
    )(module_kind, kind_scale, query, precond, train)
    return jnp.sum(parts.astype(jnp.float32), axis=0)


def solution(mesh):
    in_specs = (
        P("dp", ("section", "half")),
        P("dp", ("section", "half")),
        P(("section", "half"), None, None),
        P(("section", "half")),
        P(),
    )
    out_specs = P(("section", "half"), "dp")
    return jax.shard_map(
        per_device, mesh=mesh, in_specs=in_specs, out_specs=out_specs, check_vma=False
    )
```
